32 devices in a mesh: row: 8 (over y, x, core), col: 4 (over z).
Axes of the slice: x: 2, y: 2, z: 4, core: 2. Of those that a mesh axis runs over, the one named last changes fastest.
Arguments:
- k_blocks: bfloat16 [24, 16, 64, 64], P('row', 'col'), may hold values from -0.25 to 0.25
- p_blocks: bfloat16 [24, 16, 64, 128], P('row', 'col'), may hold values from -6 to 6
- k_columns: int32 [24, 16], P('row', 'col'), may hold values from -1 to 23, as said below
- p_columns: int32 [24, 16], P('row', 'col'), may hold values from -1 to 23, as said below
- molecule_order: int32 [24], replicated, may hold values from 0 to 23, as said below
Outputs:
- commutator: bfloat16 [24, 16, 64, 128], P('row', 'col')
The draws below stay inside these ranges and needn't reach their ends.
Inputs may be any that keep to these rules, and one draw needn't show every extreme that they name: `molecule_order`: a permutation of 0 to 23. `k_columns`: -1 marks an empty slot; the live slots 4 * g to 4 * g + 3 of a block row hold molecules whose stored block index lies in [g * 6, (g + 1) * 6); live entries of one block row are distinct; every slot of the group holding a row's own stored index is live. `p_columns`: the same rules as for k_columns, with another pattern.
All inputs are finite; a program needn't handle non-finite values.
Results may differ from the reference program's by a relative error of at most 0.001.
Values may be sent and summed in bfloat16 or wider, within the bound.
A program may use at most 128 MiB of HBM per device.

```python
import jax
import jax.numpy as jnp
from jax import lax

BLK = 64
SLOTS = 4
NBLK = 24
NGROUP = 4
ALLSLOTS = 16


def molecule_table(key):
    return jax.random.permutation(jax.random.fold_in(key, 7), NBLK).astype(jnp.int32)


def pattern_columns(key, salt):
    molecule_order = molecule_table(key)
    subkey = jax.random.fold_in(key, salt)
    key_count, key_pick, key_place = jax.random.split(subkey, 3)
    group_size = NBLK // NGROUP
    block_rows = jnp.arange(NBLK, dtype=jnp.int32)[:, None]
    group_ids = jnp.arange(NGROUP, dtype=jnp.int32)[None, :]
    home_group = block_rows // group_size
    distance = jnp.abs(group_ids - home_group)
    distance = jnp.minimum(distance, NGROUP - distance)
    live_count = jnp.where(distance <= 1, SLOTS, jax.random.randint(key_count, (NBLK, NGROUP), 0, SLOTS))
    scores = jax.random.randint(key_pick, (NBLK, NGROUP, group_size), 0, 65536) * group_size + jnp.arange(group_size, dtype=jnp.int32)
    local_cols = jnp.argsort(scores, axis=-1)[..., :SLOTS].astype(jnp.int32)
    place_scores = jax.random.randint(key_place, (NBLK, NGROUP, SLOTS), 0, 65536) * SLOTS + jnp.arange(SLOTS, dtype=jnp.int32)
    place_rank = jnp.argsort(jnp.argsort(place_scores, axis=-1), axis=-1)
    live = place_rank < live_count[..., None]
    stored = group_ids[..., None] * group_size + local_cols
    molecules = molecule_order[stored]
    return jnp.where(live, molecules, -1).astype(jnp.int32).reshape(NBLK, NGROUP * SLOTS)


def draw_molecule_order(key, part):
    return molecule_table(key)


def draw_k_columns(key, part):
    return pattern_columns(key, 11)


def draw_p_columns(key, part):
    return pattern_columns(key, 12)


def shard_levels(key, shape, pieces, low, high):
    loudness, own = 1.0, jax.random.fold_in(key, 6)
    for dim, blocks in pieces:
        draws = jnp.exp(jax.random.uniform(jax.random.fold_in(own, dim), (blocks,), jnp.float32, low / len(pieces), high / len(pieces)))
        loudness = loudness * jnp.repeat(draws, shape[dim] // blocks).reshape([-1 if axis == dim else 1 for axis in range(len(shape))])
    return loudness


def scatter_about(stream_key, extent, deviation, most, pieces=(), held_as=jnp.bfloat16):
    gain = shard_levels(stream_key, extent, pieces, -0.22, 0.18) if pieces else 1.0
    array = jax.random.normal(stream_key, extent, jnp.float32) * deviation * gain
    return jnp.minimum(jnp.maximum(array, -most), most).astype(held_as)


def setup_inputs(seed: int = 0) -> dict:
    key_list = jax.random.split(jax.random.key(seed), 6)
    k_blocks = scatter_about(key_list[0], (NBLK, ALLSLOTS, BLK, BLK), (2 * BLK * SLOTS) ** -0.5, 0.25, ((0, 8), (1, 4)))
    p_blocks = scatter_about(key_list[1], (NBLK, ALLSLOTS, BLK, 2 * BLK), 1.0, 6.0, ((0, 8), (1, 4)))
    k_columns = draw_k_columns(jax.random.fold_in(key_list[5], 71), 0)
    p_columns = draw_p_columns(jax.random.fold_in(key_list[5], 71), 0)
    molecule_order = draw_molecule_order(jax.random.fold_in(key_list[5], 71), 0)
    return dict(k_blocks=k_blocks, p_blocks=p_blocks, k_columns=k_columns, p_columns=p_columns, molecule_order=molecule_order)


def storage_of(columns, molecule_order):
    agrees = columns[..., None] == molecule_order
    position = jnp.sum(jnp.where(agrees, jnp.arange(molecule_order.shape[0], dtype=jnp.int32), 0), axis=-1).astype(jnp.int32)
    return jnp.where(columns >= 0, position, -1).astype(jnp.int32)


def select_blocks(wanted, out_columns, group_vals, group_columns):
    span_rows = group_vals.shape[0]
    slot_width = group_columns.shape[1]
    row_pick = jnp.clip(wanted, 0, span_rows - 1).astype(jnp.int32)
    row_columns = group_columns[row_pick]
    agrees = (row_columns[..., :, None] == out_columns[:, None, None, :]) & (row_columns[..., :, None] >= 0)
    slot_pick = jnp.sum(jnp.where(agrees, jnp.arange(slot_width, dtype=jnp.int32)[:, None], 0), axis=-2).astype(jnp.int32)
    matched = jnp.any(agrees, axis=-2) & (wanted >= 0)[..., None]
    flattened = group_vals.reshape((span_rows * slot_width,) + group_vals.shape[2:])
    picked = flattened[row_pick[..., None] * slot_width + slot_pick]
    return jnp.where(matched[..., None, None], picked, jnp.zeros((), picked.dtype))


def reference(k_blocks, p_blocks, k_columns, p_columns, molecule_order):
    kpos = storage_of(k_columns, molecule_order)
    ppos = storage_of(p_columns, molecule_order)

    def one_row(row_index):
        k_row = k_blocks[row_index]
        p_row = p_blocks[row_index]
        k_wanted = kpos[row_index]
        out_columns = ppos[row_index]
        slot_total = k_row.shape[0]
        block_edge = k_row.shape[1]
        out_total = out_columns.shape[0]
        p_chosen = select_blocks(k_wanted[None], out_columns[None], p_blocks, ppos)[0]
        k_chosen = select_blocks(out_columns[None], out_columns[None], k_blocks, kpos)[0]
        left_side = jnp.transpose(k_row, (1, 0, 2)).reshape(block_edge, slot_total * block_edge)
        right_side = jnp.transpose(p_chosen, (0, 2, 1, 3)).reshape(slot_total * block_edge, out_total * 2 * block_edge)
        k_then_p = jnp.dot(left_side, right_side, preferred_element_type=jnp.float32)
        k_then_p = k_then_p.reshape(block_edge, out_total, 2 * block_edge).transpose(1, 0, 2)
        p_left = p_row.reshape(slot_total, block_edge, 2, block_edge).transpose(2, 1, 0, 3).reshape(2 * block_edge, slot_total * block_edge)
        k_right = jnp.transpose(k_chosen, (0, 2, 1, 3)).reshape(slot_total * block_edge, out_total * block_edge)
        p_then_k = jnp.dot(p_left, k_right, preferred_element_type=jnp.float32)
        p_then_k = p_then_k.reshape(2, block_edge, out_total, block_edge).transpose(2, 1, 0, 3).reshape(out_total, block_edge, 2 * block_edge)
        return (k_then_p - p_then_k).astype(jnp.bfloat16)

    return lax.map(one_row, jnp.arange(NBLK, dtype=jnp.int32))
```

```python
import functools

import jax
import jax.numpy as jnp
from jax import lax
from jax.experimental import pallas as pl
from jax.experimental.pallas import tpu as pltpu
from jax.sharding import PartitionSpec as P

MESH = pl.DeviceIdType.MESH
LANES = 128
TAB = 8


def swap_halves(x):
    half = x.shape[-1] // 2
    return pltpu.roll(x.astype(jnp.float32), half, x.ndim - 1).astype(x.dtype)


def kernel(
    nrow, ncol, R, S, G,
    kc_ref, pc_ref, order_ref, k_ref, p_ref, p_any, out_ref,
    pbuf, kbuf, kcol, plcol, mrow, mcol, mrow_s, mcol_s, jout, accl, accr,
    bar_unused, s_rp, r_rp, s_rk, r_rk, s_rm, r_rm, s_ck, r_ck, s_cp, r_cp, s_cm, r_cm, lsem,
):
    r = lax.axis_index("row")
    c = lax.axis_index("col")
    H = S // 2
    PB = R * S
    KB = R * H
    SW = nrow * KB
    zero_p = nrow * PB
    zero_k = 2 * SW
    B = k_ref.shape[2]

    rows = [lax.rem(r + d, nrow) for d in range(1, nrow)]
    cols = [lax.rem(c + d, ncol) for d in range(1, ncol)]

    barrier = pltpu.get_barrier_semaphore()
    for peer in rows:
        pl.semaphore_signal(barrier, inc=1, device_id={"row": peer}, device_id_type=MESH)
    for peer in cols:
        pl.semaphore_signal(barrier, inc=1, device_id={"col": peer}, device_id_type=MESH)

    lane = lax.broadcasted_iota(jnp.int32, (1, LANES), 1)
    meta = jnp.zeros((1, LANES), jnp.int32)
    entries = []
    orders = [order_ref[c * G + j] for j in range(G)]
    krow, kcl, prow, pcl = [], [], [], []
    t_p, t_kl, t_kh = [], [], []
    for i in range(R):
        kcs = [kc_ref[i, s] for s in range(S)]
        pcs = [pc_ref[i, s] for s in range(S)]
        khit = [[kcs[s] == orders[j] for j in range(G)] for s in range(S)]
        phit = [[pcs[s] == orders[j] for j in range(G)] for s in range(S)]
        for s in range(S):
            for hit, a, b, out in ((khit, krow, kcl, False), (phit, prow, pcl, True)):
                pos_r = jnp.int32(nrow)
                pos_c = jnp.int32(0)
                col = jnp.int32(G)
                for j in range(G):
                    q = c * G + j
                    pos_r = jnp.where(hit[s][j], q // R, pos_r)
                    pos_c = jnp.where(hit[s][j], lax.rem(q, R) * TAB, pos_c)
                    col = jnp.where(hit[s][j], j, col)
                a.append(pos_r)
                b.append(pos_c)
                if out:
                    jout[i * S + s] = col
        for j in range(TAB):
            vp, vl, vh = jnp.int32(zero_p), jnp.int32(zero_k), jnp.int32(zero_k)
            if j < G:
                for s in range(S):
                    pair = (r * R + i) * H + s // 2
                    vp = jnp.where(phit[s][j], (r * R + i) * S + s, vp)
                    vl = jnp.where(khit[s][j], pair + (s % 2) * SW, vl)
                    vh = jnp.where(khit[s][j], pair + (1 - s % 2) * SW, vh)
            t_p.append(vp)
            t_kl.append(vl)
            t_kh.append(vh)
    entries = t_p + t_kl + t_kh + krow + kcl + prow + pcl
    for n, v in enumerate(entries):
        meta = jnp.where(lane == n, v, meta)
    O_KL, O_KH = R * TAB, 2 * R * TAB
    O_KR = 3 * R * TAB
    O_KC, O_PR, O_PC = O_KR + PB, O_KR + 2 * PB, O_KR + 3 * PB
    mrow[r] = meta
    mcol[c] = meta
    empty = jnp.where(lane < O_KL, zero_p, zero_k)
    mrow[nrow] = empty

    low = lax.broadcasted_iota(jnp.int32, (B, 2 * B), 1) < B
    for i in range(R):
        for h in range(H):
            pair = jnp.concatenate([k_ref[i, 2 * h], k_ref[i, 2 * h + 1]], axis=-1)
            kbuf[r * KB + i * H + h] = pair
            kcol[c, i * H + h] = pair
            a, b = p_ref[i, 2 * h], p_ref[i, 2 * h + 1]
            plcol[c, i * H + h, :B] = jnp.where(low, a, swap_halves(b))
            plcol[c, i * H + h, B:] = jnp.where(low, swap_halves(a), b)

    pl.semaphore_wait(barrier, nrow + ncol - 2)

    def row_copies(src, d, peer):
        return (
            pltpu.make_async_remote_copy(
                mrow.at[src], mrow.at[src], s_rm.at[d], r_rm.at[src],
                device_id={"row": peer}, device_id_type=MESH),
            pltpu.make_async_remote_copy(
                kbuf.at[pl.ds(src * KB, KB)], kbuf.at[pl.ds(src * KB, KB)], s_rk.at[d], r_rk.at[src],
                device_id={"row": peer}, device_id_type=MESH),
            pltpu.make_async_remote_copy(
                p_any, pbuf.at[pl.ds(src * PB, PB)], s_rp.at[d], r_rp.at[src],
                device_id={"row": peer}, device_id_type=MESH),
        )

    def col_copies(src, d, peer):
        return (
            pltpu.make_async_remote_copy(
                mcol.at[src], mcol.at[src], s_cm.at[d], r_cm.at[src],
                device_id={"col": peer}, device_id_type=MESH),
            pltpu.make_async_remote_copy(
                kcol.at[src], kcol.at[src], s_ck.at[d], r_ck.at[src],
                device_id={"col": peer}, device_id_type=MESH),
            pltpu.make_async_remote_copy(
                plcol.at[src], plcol.at[src], s_cp.at[d], r_cp.at[src],
                device_id={"col": peer}, device_id_type=MESH),
        )

    sent = [row_copies(r, d, peer) for d, peer in enumerate(rows)]
    sent_col = [col_copies(c, d, peer) for d, peer in enumerate(cols)]
    for kind in range(3):
        for cp in sent_col:
            cp[kind].start()
        for cp in sent:
            cp[kind].start()

    for i in range(R):
        for s in range(S):
            pbuf[r * PB + i * S + s] = p_ref[i, s]
    zero = jnp.zeros((B, 2 * B), jnp.bfloat16)
    pbuf[zero_p] = zero
    kbuf[zero_k] = zero
    for n in range(KB):
        kbuf[SW + r * KB + n] = swap_halves(kbuf[r * KB + n])

    for d, src in enumerate(rows):
        row_copies(src, d, src)[0].wait_recv()
    for d, src in enumerate(cols):
        col_copies(src, d, src)[0].wait_recv()
    one = pltpu.make_async_copy(mrow, mrow_s, lsem.at[0])
    two = pltpu.make_async_copy(mcol, mcol_s, lsem.at[1])
    one.start()
    two.start()
    one.wait()
    two.wait()

    for d, src in enumerate(rows):
        row_copies(src, d, src)[1].wait_recv()
        for n in range(KB):
            kbuf[SW + src * KB + n] = swap_halves(kbuf[src * KB + n])
    for d, src in enumerate(rows):
        row_copies(src, d, src)[2].wait_recv()

    def add(g, first):
        for i in range(R):
            outs = [jout[i * S + t] for t in range(S)]
            right, right_k = [], []
            for s in range(S):
                qr, qc = mcol_s[g, 0, O_KR + i * S + s], mcol_s[g, 0, O_KC + i * S + s]
                right.append(jnp.concatenate(
                    [pbuf[mrow_s[qr, 0, qc + outs[t]]] for t in range(S)], axis=1))
                qr, qc = mcol_s[g, 0, O_PR + i * S + s], mcol_s[g, 0, O_PC + i * S + s]
                right_k.append(jnp.concatenate([
                    jnp.where(low,
                              kbuf[mrow_s[qr, 0, qc + outs[2 * h] + O_KL]],
                              kbuf[mrow_s[qr, 0, qc + outs[2 * h + 1] + O_KH]])
                    for h in range(H)], axis=1))
            left = jnp.concatenate([kcol[g, i * H + h] for h in range(H)], axis=1)
            kp = jnp.dot(left, jnp.concatenate(right, axis=0), preferred_element_type=jnp.float32)
            left = jnp.concatenate([plcol[g, i * H + h] for h in range(H)], axis=1)
            pk = jnp.dot(left, jnp.concatenate(right_k, axis=0), preferred_element_type=jnp.float32)
            if first:
                accl[i] = kp
                accr[i] = pk
            else:
                accl[i] += kp
                accr[i] += pk

    add(c, True)

    def step(d, carry):
        src = lax.rem(c + d, ncol)
        for cp in col_copies(src, 0, src)[1:]:
            cp.wait_recv()
        add(src, False)
        return carry

    lax.fori_loop(1, ncol, step, 0)

    for i in range(R):
        for h in range(H):
            re = accr[i, :B, h * 2 * B:(h + 1) * 2 * B]
            im = accr[i, B:, h * 2 * B:(h + 1) * 2 * B]
            first = jnp.where(low, re, pltpu.roll(im, B, 1))
            second = jnp.where(low, pltpu.roll(re, B, 1), im)
            for t, pk in ((2 * h, first), (2 * h + 1, second)):
                out_ref[i, t] = (accl[i, :, t * 2 * B:(t + 1) * 2 * B] - pk).astype(out_ref.dtype)

    for cps in sent + sent_col:
        for cp in cps:
            cp.wait_send()


def per_device(nrow, ncol, k_blocks, p_blocks, k_columns, p_columns, molecule_order):
    R, S, B, W = p_blocks.shape
    G = molecule_order.shape[0] // ncol
    H = S // 2
    bf, i32 = jnp.bfloat16, jnp.int32
    vmem = pl.BlockSpec(memory_space=pltpu.VMEM)
    smem = pl.BlockSpec(memory_space=pltpu.SMEM)
    dma = pltpu.SemaphoreType.DMA
    return pl.pallas_call(
        functools.partial(kernel, nrow, ncol, R, S, G),
        out_shape=jax.ShapeDtypeStruct(p_blocks.shape, bf),
        in_specs=[smem, smem, smem, vmem, vmem, pl.BlockSpec(memory_space=pl.ANY)],
        out_specs=vmem,
        scratch_shapes=[
            pltpu.VMEM((nrow * R * S + 1, B, W), bf),
            pltpu.VMEM((2 * nrow * R * H + 1, B, W), bf),
            pltpu.VMEM((ncol, R * H, B, W), bf),
            pltpu.VMEM((ncol, R * H, 2 * B, W), bf),
            pltpu.VMEM((nrow + 1, 1, LANES), i32),
            pltpu.VMEM((ncol, 1, LANES), i32),
            pltpu.SMEM((nrow + 1, 1, LANES), i32),
            pltpu.SMEM((ncol, 1, LANES), i32),
            pltpu.SMEM((R * S,), i32),
            pltpu.VMEM((R, B, S * W), jnp.float32),
            pltpu.VMEM((R, 2 * B, S * B), jnp.float32),
            dma((1,)),
            dma((nrow,)), dma((nrow,)), dma((nrow,)), dma((nrow,)), dma((nrow,)), dma((nrow,)),
            dma((ncol,)), dma((ncol,)), dma((ncol,)), dma((ncol,)), dma((ncol,)), dma((ncol,)),
            dma((2,)),
        ],
        compiler_params=pltpu.CompilerParams(
            collective_id=0, has_side_effects=True, vmem_limit_bytes=48 << 20),
    )(k_columns, p_columns, molecule_order, k_blocks,
      p_blocks, p_blocks.reshape(R * S, B, W))


def solution(mesh):
    in_specs = (
        P("row", "col", None, None),
        P("row", "col", None, None),
        P("row", "col"),
        P("row", "col"),
        P(),
    )
    out_specs = P("row", "col", None, None)
    body = functools.partial(per_device, mesh.shape["row"], mesh.shape["col"])
    return jax.shard_map(
        body, mesh=mesh, in_specs=in_specs, out_specs=out_specs, check_vma=False
    )
```

```python
import functools

import jax
import jax.numpy as jnp
from jax import lax
from jax.experimental import pallas as pl
from jax.experimental.pallas import tpu as pltpu
from jax.sharding import PartitionSpec as P

MESH = pl.DeviceIdType.MESH
LANES = 128
TAB = 8


def swap_halves(x):
    half = x.shape[-1] // 2
    return pltpu.roll(x.astype(jnp.float32), half, x.ndim - 1).astype(x.dtype)


def kernel(
    nrow, ncol, R, S, G,
    kc_ref, pc_ref, order_ref, k_ref, p_ref, out_ref,
    pbuf, kbuf, kcol, plcol, mrow, mcol, mrow_s, mcol_s, jout, accl, accr,
    kc, pc, order, kv,
    s_rp, r_rp, s_rk, r_rk, s_rm, r_rm, s_fp, s_fk, s_ck, r_ck, s_cp, r_cp, s_cm, r_cm, lsem,
):
    r = lax.axis_index("row")
    c = lax.axis_index("col")
    H = S // 2
    PB = R * S
    KB = R * H
    SW = nrow * KB
    zero_p = nrow * PB
    zero_k = 2 * SW
    B = kv.shape[2]
    relay = ncol == 4

    rows = [lax.rem(r + d, nrow) for d in range(1, nrow)]
    cols = [lax.rem(c + d, ncol) for d in range(1, ncol)]
    core = lax.rem(r, 2)
    sibling = r + 1 - 2 * core
    same = [lax.rem(r + 2 * d, nrow) for d in range(1, nrow // 2)]
    other = [lax.rem(sibling + 2 * d, nrow) for d in range(1, nrow // 2)]

    barrier = pltpu.get_barrier_semaphore()
    for peer in rows:
        pl.semaphore_signal(barrier, inc=1, device_id={"row": peer}, device_id_type=MESH)
    for peer in cols:
        pl.semaphore_signal(barrier, inc=1, device_id={"col": peer}, device_id_type=MESH)

    loads = [
        pltpu.make_async_copy(src, dst, lsem.at[n])
        for n, (src, dst) in enumerate((
            (kc_ref, kc), (pc_ref, pc), (order_ref, order), (k_ref, kv),
            (p_ref, pbuf.at[pl.ds(r * PB, PB)])))
    ]
    for cp in loads:
        cp.start()
    for cp in loads[:3]:
        cp.wait()

    lane = lax.broadcasted_iota(jnp.int32, (1, LANES), 1)
    meta = jnp.zeros((1, LANES), jnp.int32)
    orders = [order[c * G + j] for j in range(G)]
    krow, kcl, prow, pcl = [], [], [], []
    t_p, t_kl, t_kh = [], [], []
    for i in range(R):
        kcs = [kc[i, s] for s in range(S)]
        pcs = [pc[i, s] for s in range(S)]
        khit = [[kcs[s] == orders[j] for j in range(G)] for s in range(S)]
        phit = [[pcs[s] == orders[j] for j in range(G)] for s in range(S)]
        for s in range(S):
            for hit, a, b, out in ((khit, krow, kcl, False), (phit, prow, pcl, True)):
                pos_r = jnp.int32(nrow)
                pos_c = jnp.int32(0)
                col = jnp.int32(G)
                for j in range(G):
                    q = c * G + j
                    pos_r = jnp.where(hit[s][j], q // R, pos_r)
                    pos_c = jnp.where(hit[s][j], lax.rem(q, R) * TAB, pos_c)
                    col = jnp.where(hit[s][j], j, col)
                a.append(pos_r)
                b.append(pos_c)
                if out:
                    jout[i * S + s] = col
        for j in range(TAB):
            vp, vl, vh = jnp.int32(zero_p), jnp.int32(zero_k), jnp.int32(zero_k)
            if j < G:
                for s in range(S):
                    pair = (r * R + i) * H + s // 2
                    vp = jnp.where(phit[s][j], (r * R + i) * S + s, vp)
                    vl = jnp.where(khit[s][j], pair + (s % 2) * SW, vl)
                    vh = jnp.where(khit[s][j], pair + (1 - s % 2) * SW, vh)
            t_p.append(vp)
            t_kl.append(vl)
            t_kh.append(vh)
    entries = t_p + t_kl + t_kh + krow + kcl + prow + pcl
    for n, v in enumerate(entries):
        meta = jnp.where(lane == n, v, meta)
    O_KL, O_KH = R * TAB, 2 * R * TAB
    O_KR = 3 * R * TAB
    O_KC, O_PR, O_PC = O_KR + PB, O_KR + 2 * PB, O_KR + 3 * PB
    mrow[r] = meta
    mcol[c] = meta
    mrow[nrow] = jnp.where(lane < O_KL, zero_p, zero_k)

    for cp in loads[3:]:
        cp.wait()
    low = lax.broadcasted_iota(jnp.int32, (B, 2 * B), 1) < B
    for i in range(R):
        for h in range(H):
            pair = jnp.concatenate([kv[i, 2 * h], kv[i, 2 * h + 1]], axis=-1)
            kbuf[r * KB + i * H + h] = pair
            kcol[c, i * H + h] = pair
            a, b = pbuf[r * PB + i * S + 2 * h], pbuf[r * PB + i * S + 2 * h + 1]
            plcol[c, i * H + h, :B] = jnp.where(low, a, swap_halves(b))
            plcol[c, i * H + h, B:] = jnp.where(low, swap_halves(a), b)

    pl.semaphore_wait(barrier, nrow + ncol - 2)

    def row_copy(kind, src, send, peer):
        ref, recv = (
            (mrow.at[src], r_rm), (kbuf.at[pl.ds(src * KB, KB)], r_rk), (pbuf.at[pl.ds(src * PB, PB)], r_rp)
        )[kind]
        return pltpu.make_async_remote_copy(
            ref, ref, send, recv.at[src], device_id={"row": peer}, device_id_type=MESH)

    def col_copy(kind, src, send, peer):
        ref, recv = ((mcol, r_cm), (kcol, r_ck), (plcol, r_cp))[kind]
        return pltpu.make_async_remote_copy(
            ref.at[src], ref.at[src], send, recv.at[src], device_id={"col": peer}, device_id_type=MESH)

    def row_got(kind, src):
        row_copy(kind, src, s_rm.at[0], src).wait_recv()

    def col_got(kind, src):
        col_copy(kind, src, s_cm.at[0], src).wait_recv()

    sent = []

    def start(cp):
        cp.start()
        sent.append(cp)

    for d, peer in enumerate(cols):
        start(col_copy(0, c, s_cm.at[d], peer))
    for d, peer in enumerate(rows):
        start(row_copy(0, r, s_rm.at[d], peer))
    if relay:
        inner = (c == 1) | (c == 2)
        mirror = jnp.where(c < 2, 1, -1)
        plan = [c + 2 * mirror, c + mirror]
        for d, peer in enumerate(plan):
            for kind in (1, 2):
                start(col_copy(kind, c, (s_ck, s_cp)[kind - 1].at[d], peer))

        @pl.when(inner)
        def _():
            for kind in (1, 2):
                col_copy(kind, c, (s_ck, s_cp)[kind - 1].at[2], c - mirror).start()
    else:
        for d, peer in enumerate(cols):
            for kind in (1, 2):
                start(col_copy(kind, c, (s_ck, s_cp)[kind - 1].at[d], peer))
    for kind in (1, 2):
        for d, peer in enumerate(same + [sibling]):
            start(row_copy(kind, r, (s_rk, s_rp)[kind - 1].at[d], peer))

    zero = jnp.zeros((B, 2 * B), jnp.bfloat16)
    pbuf[zero_p] = zero
    kbuf[zero_k] = zero

    def swapped(src):
        for n in range(KB):
            kbuf[SW + src * KB + n] = swap_halves(kbuf[src * KB + n])

    swapped(r)

    for src in rows:
        row_got(0, src)
    for src in cols:
        col_got(0, src)
    tables = [pltpu.make_async_copy(mrow, mrow_s, lsem.at[0]), pltpu.make_async_copy(mcol, mcol_s, lsem.at[1])]
    for cp in tables:
        cp.start()
    for cp in tables:
        cp.wait()

    for d, src in enumerate(same):
        row_got(1, src)
        start(row_copy(1, src, s_fk.at[d], sibling))
        swapped(src)
    if relay:
        @pl.when(inner)
        def _():
            for kind in (1, 2):
                col_got(kind, jnp.where(c == 1, 3, 0))
                col_copy(kind, jnp.where(c == 1, 3, 0), (s_ck, s_cp)[kind - 1].at[3], c - mirror).start()
    for d, src in enumerate(same):
        row_got(2, src)
        start(row_copy(2, src, s_fp.at[d], sibling))
    for src in [sibling] + other:
        row_got(1, src)
        swapped(src)
    for src in [sibling] + other:
        row_got(2, src)

    def add(g, first):
        for i in range(R):
            outs = [jout[i * S + t] for t in range(S)]
            right, right_k = [], []
            for s in range(S):
                qr, qc = mcol_s[g, 0, O_KR + i * S + s], mcol_s[g, 0, O_KC + i * S + s]
                right.append(jnp.concatenate(
                    [pbuf[mrow_s[qr, 0, qc + outs[t]]] for t in range(S)], axis=1))
                qr, qc = mcol_s[g, 0, O_PR + i * S + s], mcol_s[g, 0, O_PC + i * S + s]
                right_k.append(jnp.concatenate([
                    jnp.where(low,
                              kbuf[mrow_s[qr, 0, qc + outs[2 * h] + O_KL]],
                              kbuf[mrow_s[qr, 0, qc + outs[2 * h + 1] + O_KH]])
                    for h in range(H)], axis=1))
            left = jnp.concatenate([kcol[g, i * H + h] for h in range(H)], axis=1)
            kp = jnp.dot(left, jnp.concatenate(right, axis=0), preferred_element_type=jnp.float32)
            left = jnp.concatenate([plcol[g, i * H + h] for h in range(H)], axis=1)
            pk = jnp.dot(left, jnp.concatenate(right_k, axis=0), preferred_element_type=jnp.float32)
            if first:
                accl[i] = kp
                accr[i] = pk
            else:
                accl[i] += kp
                accr[i] += pk

    add(c, True)

    def step(d, carry):
        if relay:
            src = lax.rem(c + mirror * d + ncol, ncol)
            taken = inner & (src == jnp.where(c == 1, 3, 0))

            @pl.when(jnp.logical_not(taken))
            def _():
                col_got(1, src)
                col_got(2, src)
        else:
            src = lax.rem(c + d, ncol)
            col_got(1, src)
            col_got(2, src)
        add(src, False)
        return carry

    lax.fori_loop(1, ncol, step, 0)

    for i in range(R):
        for h in range(H):
            re = accr[i, :B, h * 2 * B:(h + 1) * 2 * B]
            im = accr[i, B:, h * 2 * B:(h + 1) * 2 * B]
            first = jnp.where(low, re, pltpu.roll(im, B, 1))
            second = jnp.where(low, pltpu.roll(re, B, 1), im)
            for t, pk in ((2 * h, first), (2 * h + 1, second)):
                out_ref[i, t] = (accl[i, :, t * 2 * B:(t + 1) * 2 * B] - pk).astype(out_ref.dtype)

    for cp in sent:
        cp.wait_send()
    if relay:
        @pl.when(inner)
        def _():
            for kind in (1, 2):
                for n in (2, 3):
                    col_copy(kind, c, (s_ck, s_cp)[kind - 1].at[n], c - mirror).wait_send()


def per_device(nrow, ncol, k_blocks, p_blocks, k_columns, p_columns, molecule_order):
    R, S, B, W = p_blocks.shape
    G = molecule_order.shape[0] // ncol
    H = S // 2
    bf, i32 = jnp.bfloat16, jnp.int32
    vmem = pl.BlockSpec(memory_space=pltpu.VMEM)
    anywhere = pl.BlockSpec(memory_space=pl.ANY)
    dma = pltpu.SemaphoreType.DMA
    return pl.pallas_call(
        functools.partial(kernel, nrow, ncol, R, S, G),
        out_shape=jax.ShapeDtypeStruct(p_blocks.shape, bf),
        in_specs=[anywhere] * 5,
        out_specs=vmem,
        scratch_shapes=[
            pltpu.VMEM((nrow * R * S + 1, B, W), bf),
            pltpu.VMEM((2 * nrow * R * H + 1, B, W), bf),
            pltpu.VMEM((ncol, R * H, B, W), bf),
            pltpu.VMEM((ncol, R * H, 2 * B, W), bf),
            pltpu.VMEM((nrow + 1, 1, LANES), i32),
            pltpu.VMEM((ncol, 1, LANES), i32),
            pltpu.SMEM((nrow + 1, 1, LANES), i32),
            pltpu.SMEM((ncol, 1, LANES), i32),
            pltpu.SMEM((R * S,), i32),
            pltpu.VMEM((R, B, S * W), jnp.float32),
            pltpu.VMEM((R, 2 * B, S * B), jnp.float32),
            pltpu.SMEM((R, S), i32),
            pltpu.SMEM((R, S), i32),
            pltpu.SMEM(molecule_order.shape, i32),
            pltpu.VMEM((R, S, B, B), bf),
            *[dma((nrow,))] * 8,
            *[dma((ncol,))] * 6,
            dma((5,)),
        ],
        compiler_params=pltpu.CompilerParams(
            collective_id=0, has_side_effects=True, vmem_limit_bytes=48 << 20),
    )(k_columns, p_columns, molecule_order, k_blocks,
      p_blocks.reshape(R * S, B, W))


def solution(mesh):
    in_specs = (
        P("row", "col", None, None),
        P("row", "col", None, None),
        P("row", "col"),
        P("row", "col"),
        P(),
    )
    out_specs = P("row", "col", None, None)
    body = functools.partial(per_device, mesh.shape["row"], mesh.shape["col"])
    return jax.shard_map(
        body, mesh=mesh, in_specs=in_specs, out_specs=out_specs, check_vma=False
    )
```

```python
import functools

import jax
import jax.numpy as jnp
from jax import lax
from jax.experimental import pallas as pl
from jax.experimental.pallas import tpu as pltpu
from jax.sharding import PartitionSpec as P

MESH = pl.DeviceIdType.MESH
LANES = 128
TAB = 8


def swap_halves(x):
    half = x.shape[-1] // 2
    return pltpu.roll(x.astype(jnp.float32), half, x.ndim - 1).astype(x.dtype)


def kernel(
    nrow, ncol, R, S, G,
    kc_ref, pc_ref, order_ref, k_ref, p_ref, out_ref,
    pbuf, kbuf, kcol, plcol, mrow, mcol, mrow_s, mcol_s, jout, accl, accr,
    kc, pc, order, kv,
    s_rp, r_rp, s_rk, r_rk, s_rm, r_rm, s_fp, s_fk, s_ck, r_ck, s_cp, r_cp, s_cm, r_cm, lsem,
):
    r = lax.axis_index("row")
    c = lax.axis_index("col")
    H = S // 2
    PB = R * S
    KB = R * H
    SW = nrow * KB
    zero_p = nrow * PB
    zero_k = 2 * SW
    B = kv.shape[2]
    relay = ncol == 4

    rows = [lax.rem(r + d, nrow) for d in range(1, nrow)]
    cols = [lax.rem(c + d, ncol) for d in range(1, ncol)]
    core = lax.rem(r, 2)
    sibling = r + 1 - 2 * core
    same = [lax.rem(r + 2 * d, nrow) for d in range(1, nrow // 2)]
    other = [lax.rem(sibling + 2 * d, nrow) for d in range(1, nrow // 2)]

    barrier = pltpu.get_barrier_semaphore()
    for peer in rows:
        pl.semaphore_signal(barrier, inc=1, device_id={"row": peer}, device_id_type=MESH)
    for peer in cols:
        pl.semaphore_signal(barrier, inc=1, device_id={"col": peer}, device_id_type=MESH)

    loads = [
        pltpu.make_async_copy(src, dst, lsem.at[n])
        for n, (src, dst) in enumerate((
            (kc_ref, kc), (pc_ref, pc), (order_ref, order), (k_ref, kv),
            (p_ref, pbuf.at[pl.ds(r * PB, PB)])))
    ]
    for cp in loads:
        cp.start()

    for cp in loads[:3]:
        cp.wait()

    lane = lax.broadcasted_iota(jnp.int32, (1, LANES), 1)
    meta = jnp.zeros((1, LANES), jnp.int32)
    orders = [order[c * G + j] for j in range(G)]
    krow, kcl, prow, pcl = [], [], [], []
    t_p, t_kl, t_kh = [], [], []
    for i in range(R):
        kcs = [kc[i, s] for s in range(S)]
        pcs = [pc[i, s] for s in range(S)]
        khit = [[kcs[s] == orders[j] for j in range(G)] for s in range(S)]
        phit = [[pcs[s] == orders[j] for j in range(G)] for s in range(S)]
        for s in range(S):
            for hit, a, b, out in ((khit, krow, kcl, False), (phit, prow, pcl, True)):
                pos_r = jnp.int32(nrow)
                pos_c = jnp.int32(0)
                col = jnp.int32(G)
                for j in range(G):
                    q = c * G + j
                    pos_r = jnp.where(hit[s][j], q // R, pos_r)
                    pos_c = jnp.where(hit[s][j], lax.rem(q, R) * TAB, pos_c)
                    col = jnp.where(hit[s][j], j, col)
                a.append(pos_r)
                b.append(pos_c)
                if out:
                    jout[i * S + s] = col
        for j in range(TAB):
            vp, vl, vh = jnp.int32(zero_p), jnp.int32(zero_k), jnp.int32(zero_k)
            if j < G:
                for s in range(S):
                    pair = (r * R + i) * H + s // 2
                    vp = jnp.where(phit[s][j], (r * R + i) * S + s, vp)
                    vl = jnp.where(khit[s][j], pair + (s % 2) * SW, vl)
                    vh = jnp.where(khit[s][j], pair + (1 - s % 2) * SW, vh)
            t_p.append(vp)
            t_kl.append(vl)
            t_kh.append(vh)
    entries = t_p + t_kl + t_kh + krow + kcl + prow + pcl
    for n, v in enumerate(entries):
        meta = jnp.where(lane == n, v, meta)
    O_KL, O_KH = R * TAB, 2 * R * TAB
    O_KR = 3 * R * TAB
    O_KC, O_PR, O_PC = O_KR + PB, O_KR + 2 * PB, O_KR + 3 * PB
    mrow[r] = meta
    mcol[c] = meta
    mrow[nrow] = jnp.where(lane < O_KL, zero_p, zero_k)

    for cp in loads[3:]:
        cp.wait()
    low = lax.broadcasted_iota(jnp.int32, (B, 2 * B), 1) < B
    for i in range(R):
        for h in range(H):
            pair = jnp.concatenate([kv[i, 2 * h], kv[i, 2 * h + 1]], axis=-1)
            kbuf[r * KB + i * H + h] = pair
            kcol[c, i * H + h] = pair
            a, b = pbuf[r * PB + i * S + 2 * h], pbuf[r * PB + i * S + 2 * h + 1]
            plcol[c, i * H + h, :B] = jnp.where(low, a, swap_halves(b))
            plcol[c, i * H + h, B:] = jnp.where(low, swap_halves(a), b)

    pl.semaphore_wait(barrier, nrow + ncol - 2)

    def row_copy(kind, src, send, peer):
        ref, recv = (
            (mrow.at[src], r_rm), (kbuf.at[pl.ds(src * KB, KB)], r_rk), (pbuf.at[pl.ds(src * PB, PB)], r_rp)
        )[kind]
        return pltpu.make_async_remote_copy(
            ref, ref, send, recv.at[src], device_id={"row": peer}, device_id_type=MESH)

    def col_copy(kind, src, send, peer):
        ref, recv = ((mcol, r_cm), (kcol, r_ck), (plcol, r_cp))[kind]
        return pltpu.make_async_remote_copy(
            ref.at[src], ref.at[src], send, recv.at[src], device_id={"col": peer}, device_id_type=MESH)

    def row_got(kind, src):
        row_copy(kind, src, s_rm.at[0], src).wait_recv()

    def col_got(kind, src):
        col_copy(kind, src, s_cm.at[0], src).wait_recv()

    sent = []

    def start(cp):
        cp.start()
        sent.append(cp)

    for d, peer in enumerate(cols):
        start(col_copy(0, c, s_cm.at[d], peer))
    for d, peer in enumerate(rows):
        start(row_copy(0, r, s_rm.at[d], peer))
    if relay:
        inner = (c == 1) | (c == 2)
        mirror = jnp.where(c < 2, 1, -1)
        plan = [c + 2 * mirror, c + mirror]
        for d, peer in enumerate(plan):
            for kind in (1, 2):
                start(col_copy(kind, c, (s_ck, s_cp)[kind - 1].at[d], peer))

        @pl.when(inner)
        def _():
            for kind in (1, 2):
                col_copy(kind, c, (s_ck, s_cp)[kind - 1].at[2], c - mirror).start()
    else:
        for d, peer in enumerate(cols):
            for kind in (1, 2):
                start(col_copy(kind, c, (s_ck, s_cp)[kind - 1].at[d], peer))
    for kind in (1, 2):
        for d, peer in enumerate(same + [sibling]):
            start(row_copy(kind, r, (s_rk, s_rp)[kind - 1].at[d], peer))

    zero = jnp.zeros((B, 2 * B), jnp.bfloat16)
    pbuf[zero_p] = zero
    kbuf[zero_k] = zero

    def swapped(src):
        for n in range(KB):
            kbuf[SW + src * KB + n] = swap_halves(kbuf[src * KB + n])

    swapped(r)

    if relay:
        @pl.when(inner)
        def _():
            for kind in (1, 2):
                col_got(kind, jnp.where(c == 1, 3, 0))
                col_copy(kind, jnp.where(c == 1, 3, 0), (s_ck, s_cp)[kind - 1].at[3], c - mirror).start()
    for d, src in enumerate(same):
        row_got(1, src)
        start(row_copy(1, src, s_fk.at[d], sibling))
        swapped(src)
    for d, src in enumerate(same):
        row_got(2, src)
        start(row_copy(2, src, s_fp.at[d], sibling))
    for src in [sibling] + other:
        row_got(1, src)
        swapped(src)
    for src in [sibling] + other:
        row_got(2, src)

    for src in rows:
        row_got(0, src)
    for src in cols:
        col_got(0, src)
    tables = [pltpu.make_async_copy(mrow, mrow_s, lsem.at[0]), pltpu.make_async_copy(mcol, mcol_s, lsem.at[1])]
    for cp in tables:
        cp.start()
    for cp in tables:
        cp.wait()

    def add(g, first):
        for i in range(R):
            outs = [jout[i * S + t] for t in range(S)]
            right, right_k = [], []
            for s in range(S):
                qr, qc = mcol_s[g, 0, O_KR + i * S + s], mcol_s[g, 0, O_KC + i * S + s]
                right.append(jnp.concatenate(
                    [pbuf[mrow_s[qr, 0, qc + outs[t]]] for t in range(S)], axis=1))
                qr, qc = mcol_s[g, 0, O_PR + i * S + s], mcol_s[g, 0, O_PC + i * S + s]
                right_k.append(jnp.concatenate([
                    jnp.where(low,
                              kbuf[mrow_s[qr, 0, qc + outs[2 * h] + O_KL]],
                              kbuf[mrow_s[qr, 0, qc + outs[2 * h + 1] + O_KH]])
                    for h in range(H)], axis=1))
            left = jnp.concatenate([kcol[g, i * H + h] for h in range(H)], axis=1)
            kp = jnp.dot(left, jnp.concatenate(right, axis=0), preferred_element_type=jnp.float32)
            left = jnp.concatenate([plcol[g, i * H + h] for h in range(H)], axis=1)
            pk = jnp.dot(left, jnp.concatenate(right_k, axis=0), preferred_element_type=jnp.float32)
            if first:
                accl[i] = kp
                accr[i] = pk
            else:
                accl[i] += kp
                accr[i] += pk

    add(c, True)

    def step(d, carry):
        if relay:
            src = lax.rem(c + mirror * d + ncol, ncol)
            taken = inner & (src == jnp.where(c == 1, 3, 0))

            @pl.when(jnp.logical_not(taken))
            def _():
                col_got(1, src)
                col_got(2, src)
        else:
            src = lax.rem(c + d, ncol)
            col_got(1, src)
            col_got(2, src)
        add(src, False)
        return carry

    lax.fori_loop(1, ncol, step, 0)

    for i in range(R):
        for h in range(H):
            re = accr[i, :B, h * 2 * B:(h + 1) * 2 * B]
            im = accr[i, B:, h * 2 * B:(h + 1) * 2 * B]
            first = jnp.where(low, re, pltpu.roll(im, B, 1))
            second = jnp.where(low, pltpu.roll(re, B, 1), im)
            for t, pk in ((2 * h, first), (2 * h + 1, second)):
                out_ref[i, t] = (accl[i, :, t * 2 * B:(t + 1) * 2 * B] - pk).astype(out_ref.dtype)

    for cp in sent:
        cp.wait_send()
    if relay:
        @pl.when(inner)
        def _():
            for kind in (1, 2):
                for n in (2, 3):
                    col_copy(kind, c, (s_ck, s_cp)[kind - 1].at[n], c - mirror).wait_send()


def per_device(nrow, ncol, k_blocks, p_blocks, k_columns, p_columns, molecule_order):
    R, S, B, W = p_blocks.shape
    G = molecule_order.shape[0] // ncol
    H = S // 2
    bf, i32 = jnp.bfloat16, jnp.int32
    vmem = pl.BlockSpec(memory_space=pltpu.VMEM)
    anywhere = pl.BlockSpec(memory_space=pltpu.HBM)
    dma = pltpu.SemaphoreType.DMA
    return pl.pallas_call(
        functools.partial(kernel, nrow, ncol, R, S, G),
        out_shape=jax.ShapeDtypeStruct(p_blocks.shape, bf),
        in_specs=[anywhere] * 5,
        out_specs=vmem,
        scratch_shapes=[
            pltpu.VMEM((nrow * R * S + 1, B, W), bf),
            pltpu.VMEM((2 * nrow * R * H + 1, B, W), bf),
            pltpu.VMEM((ncol, R * H, B, W), bf),
            pltpu.VMEM((ncol, R * H, 2 * B, W), bf),
            pltpu.VMEM((nrow + 1, 1, LANES), i32),
            pltpu.VMEM((ncol, 1, LANES), i32),
            pltpu.SMEM((nrow + 1, 1, LANES), i32),
            pltpu.SMEM((ncol, 1, LANES), i32),
            pltpu.SMEM((R * S,), i32),
            pltpu.VMEM((R, B, S * W), jnp.float32),
            pltpu.VMEM((R, 2 * B, S * B), jnp.float32),
            pltpu.SMEM((R, S), i32),
            pltpu.SMEM((R, S), i32),
            pltpu.SMEM(molecule_order.shape, i32),
            pltpu.VMEM((R, S, B, B), bf),
            *[dma((nrow,))] * 8,
            *[dma((ncol,))] * 6,
            dma((5,)),
        ],
        compiler_params=pltpu.CompilerParams(
            collective_id=0, has_side_effects=True, vmem_limit_bytes=60 << 20),
    )(k_columns, p_columns, molecule_order, k_blocks,
      p_blocks.reshape(R * S, B, W))


def solution(mesh):
    in_specs = (
        P("row", "col", None, None),
        P("row", "col", None, None),
        P("row", "col"),
        P("row", "col"),
        P(),
    )
    out_specs = P("row", "col", None, None)
    body = functools.partial(per_device, mesh.shape["row"], mesh.shape["col"])
    return jax.shard_map(
        body, mesh=mesh, in_specs=in_specs, out_specs=out_specs, check_vma=False
    )
```

```python
import functools

import jax
import jax.numpy as jnp
from jax import lax
from jax.experimental import pallas as pl
from jax.experimental.pallas import tpu as pltpu
from jax.sharding import PartitionSpec as P

MESH = pl.DeviceIdType.MESH
LANES = 128
TAB = 8


def swap_halves(x):
    half = x.shape[-1] // 2
    return pltpu.roll(x.astype(jnp.float32), half, x.ndim - 1).astype(x.dtype)


def kernel(
    nrow, ncol, R, S, G,
    kc_ref, pc_ref, order_ref, k_ref, p_ref, out_ref,
    pbuf, kbuf, kcol, plcol, mrow, mcol, mrow_s, mcol_s, jout, accl, accr,
    kc, pc, order, kv,
    s_rp, r_rp, s_rk, r_rk, s_rm, r_rm, s_fm, s_fp, s_fk, s_ck, r_ck, s_cp, r_cp, s_cm, r_cm, lsem,
):
    r = lax.axis_index("row")
    c = lax.axis_index("col")
    H = S // 2
    PB = R * S
    KB = R * H
    SW = nrow * KB
    zero_p = nrow * PB
    zero_k = 2 * SW
    B = kv.shape[2]
    relay = ncol == 4

    rows = [lax.rem(r + d, nrow) for d in range(1, nrow)]
    cols = [lax.rem(c + d, ncol) for d in range(1, ncol)]
    core = lax.rem(r, 2)
    sibling = r + 1 - 2 * core
    same = [lax.rem(r + 2 * d, nrow) for d in range(1, nrow // 2)]
    other = [lax.rem(sibling + 2 * d, nrow) for d in range(1, nrow // 2)]

    barrier = pltpu.get_barrier_semaphore()
    near = same + [sibling] if relay else rows
    for peer in near:
        pl.semaphore_signal(barrier, inc=1, device_id={"row": peer}, device_id_type=MESH)
    if relay:
        inner = (c == 1) | (c == 2)
        mirror = jnp.where(c < 2, 1, -1)
        far = jnp.where(c == 1, 3, 0)
        has = (c < ncol - 1, c > 0)
        step_to = (c + 1, c - 1)
        arrivals = len(near) + jnp.where(inner, 2, 1)
        for ok, peer in zip(has, step_to):
            @pl.when(ok)
            def _(peer=peer):
                pl.semaphore_signal(barrier, inc=1, device_id={"col": peer}, device_id_type=MESH)
    else:
        arrivals = nrow + ncol - 2
        for peer in cols:
            pl.semaphore_signal(barrier, inc=1, device_id={"col": peer}, device_id_type=MESH)

    loads = [
        pltpu.make_async_copy(src, dst, lsem.at[n])
        for n, (src, dst) in enumerate((
            (kc_ref, kc), (pc_ref, pc), (order_ref, order), (k_ref, kv),
            (p_ref, pbuf.at[pl.ds(r * PB, PB)])))
    ]
    for cp in loads:
        cp.start()

    for cp in loads[:3]:
        cp.wait()

    lane = lax.broadcasted_iota(jnp.int32, (1, LANES), 1)
    meta = jnp.zeros((1, LANES), jnp.int32)
    orders = [order[c * G + j] for j in range(G)]
    krow, kcl, prow, pcl = [], [], [], []
    t_p, t_kl, t_kh = [], [], []
    for i in range(R):
        kcs = [kc[i, s] for s in range(S)]
        pcs = [pc[i, s] for s in range(S)]
        khit = [[kcs[s] == orders[j] for j in range(G)] for s in range(S)]
        phit = [[pcs[s] == orders[j] for j in range(G)] for s in range(S)]
        for s in range(S):
            for hit, a, b, out in ((khit, krow, kcl, False), (phit, prow, pcl, True)):
                pos_r = jnp.int32(nrow)
                pos_c = jnp.int32(0)
                col = jnp.int32(G)
                for j in range(G):
                    q = c * G + j
                    pos_r = jnp.where(hit[s][j], q // R, pos_r)
                    pos_c = jnp.where(hit[s][j], lax.rem(q, R) * TAB, pos_c)
                    col = jnp.where(hit[s][j], j, col)
                a.append(pos_r)
                b.append(pos_c)
                if out:
                    jout[i * S + s] = col
        for j in range(TAB):
            vp, vl, vh = jnp.int32(zero_p), jnp.int32(zero_k), jnp.int32(zero_k)
            if j < G:
                for s in range(S):
                    pair = (r * R + i) * H + s // 2
                    vp = jnp.where(phit[s][j], (r * R + i) * S + s, vp)
                    vl = jnp.where(khit[s][j], pair + (s % 2) * SW, vl)
                    vh = jnp.where(khit[s][j], pair + (1 - s % 2) * SW, vh)
            t_p.append(vp)
            t_kl.append(vl)
            t_kh.append(vh)
    entries = t_p + t_kl + t_kh + krow + kcl + prow + pcl
    for n, v in enumerate(entries):
        meta = jnp.where(lane == n, v, meta)
    O_KL, O_KH = R * TAB, 2 * R * TAB
    O_KR = 3 * R * TAB
    O_KC, O_PR, O_PC = O_KR + PB, O_KR + 2 * PB, O_KR + 3 * PB
    mrow[r] = meta
    mcol[c] = meta
    mrow[nrow] = jnp.where(lane < O_KL, zero_p, zero_k)

    for cp in loads[3:]:
        cp.wait()
    low = lax.broadcasted_iota(jnp.int32, (B, 2 * B), 1) < B
    for i in range(R):
        for h in range(H):
            pair = jnp.concatenate([kv[i, 2 * h], kv[i, 2 * h + 1]], axis=-1)
            kbuf[r * KB + i * H + h] = pair
            kcol[c, i * H + h] = pair
            a, b = pbuf[r * PB + i * S + 2 * h], pbuf[r * PB + i * S + 2 * h + 1]
            plcol[c, i * H + h, :B] = jnp.where(low, a, swap_halves(b))
            plcol[c, i * H + h, B:] = jnp.where(low, swap_halves(a), b)

    pl.semaphore_wait(barrier, arrivals)

    def row_copy(kind, src, send, peer):
        ref, recv = (
            (mrow.at[src], r_rm), (kbuf.at[pl.ds(src * KB, KB)], r_rk), (pbuf.at[pl.ds(src * PB, PB)], r_rp)
        )[kind]
        return pltpu.make_async_remote_copy(
            ref, ref, send, recv.at[src], device_id={"row": peer}, device_id_type=MESH)

    def col_copy(kind, src, send, peer):
        ref, recv = ((mcol, r_cm), (kcol, r_ck), (plcol, r_cp))[kind]
        return pltpu.make_async_remote_copy(
            ref.at[src], ref.at[src], send, recv.at[src], device_id={"col": peer}, device_id_type=MESH)

    def row_got(kind, src):
        row_copy(kind, src, s_rm.at[0], src).wait_recv()

    def col_got(kind, src):
        col_copy(kind, src, s_cm.at[0], src).wait_recv()

    sent = []

    def start(cp):
        cp.start()
        sent.append(cp)

    col_sems = (s_cm, s_ck, s_cp)

    def pass_on(kind, src, slot, peer):
        return col_copy(kind, src, col_sems[kind].at[slot], peer)

    if relay:
        for kind in range(3):
            for n, (ok, peer) in enumerate(zip(has, step_to)):
                @pl.when(ok)
                def _(kind=kind, n=n, peer=peer):
                    pass_on(kind, c, n, peer).start()
            for d, peer in enumerate(near):
                start(row_copy(kind, r, (s_rm, s_rk, s_rp)[kind].at[d], peer))
    else:
        for kind in range(3):
            for d, peer in enumerate(cols):
                start(pass_on(kind, c, d, peer))
            for d, peer in enumerate(same + [sibling] if kind else rows):
                start(row_copy(kind, r, (s_rm, s_rk, s_rp)[kind].at[d], peer))

    zero = jnp.zeros((B, 2 * B), jnp.bfloat16)
    pbuf[zero_p] = zero
    kbuf[zero_k] = zero

    def swapped(src):
        for n in range(KB):
            kbuf[SW + src * KB + n] = swap_halves(kbuf[src * KB + n])

    swapped(r)

    def inside(kinds, hops):
        if relay:
            @pl.when(inner)
            def _():
                for kind in kinds:
                    for src, slot, peer in hops:
                        col_got(kind, src)
                        pass_on(kind, src, slot, peer).start()

    if relay:
        onward = [(c - 1, 2, c + 1), (c + 1, 3, c - 1)]
        last = [(far, 4, c - mirror)]
    else:
        onward = last = []
    inside((0, 1), onward)
    for d, src in enumerate(same):
        if relay:
            row_got(0, src)
            start(row_copy(0, src, s_fm.at[d], sibling))
        row_got(1, src)
        start(row_copy(1, src, s_fk.at[d], sibling))
    inside((2,), onward)
    for src in same:
        swapped(src)
    inside((0, 1), last)
    for d, src in enumerate(same):
        row_got(2, src)
        start(row_copy(2, src, s_fp.at[d], sibling))
    inside((2,), last)
    for src in [sibling] + other:
        row_got(1, src)
        swapped(src)
    for src in [sibling] + other:
        row_got(2, src)

    for src in [sibling] + other if relay else rows:
        row_got(0, src)
    if relay:
        @pl.when(jnp.logical_not(inner))
        def _():
            for d in range(1, ncol):
                col_got(0, c + mirror * d)
    else:
        for src in cols:
            col_got(0, src)
    tables = [pltpu.make_async_copy(mrow, mrow_s, lsem.at[0]), pltpu.make_async_copy(mcol, mcol_s, lsem.at[1])]
    for cp in tables:
        cp.start()
    for cp in tables:
        cp.wait()

    def add(g, first):
        for i in range(R):
            outs = [jout[i * S + t] for t in range(S)]
            right, right_k = [], []
            for s in range(S):
                qr, qc = mcol_s[g, 0, O_KR + i * S + s], mcol_s[g, 0, O_KC + i * S + s]
                right.append(jnp.concatenate(
                    [pbuf[mrow_s[qr, 0, qc + outs[t]]] for t in range(S)], axis=1))
                qr, qc = mcol_s[g, 0, O_PR + i * S + s], mcol_s[g, 0, O_PC + i * S + s]
                right_k.append(jnp.concatenate([
                    jnp.where(low,
                              kbuf[mrow_s[qr, 0, qc + outs[2 * h] + O_KL]],
                              kbuf[mrow_s[qr, 0, qc + outs[2 * h + 1] + O_KH]])
                    for h in range(H)], axis=1))
            left = jnp.concatenate([kcol[g, i * H + h] for h in range(H)], axis=1)
            kp = jnp.dot(left, jnp.concatenate(right, axis=0), preferred_element_type=jnp.float32)
            left = jnp.concatenate([plcol[g, i * H + h] for h in range(H)], axis=1)
            pk = jnp.dot(left, jnp.concatenate(right_k, axis=0), preferred_element_type=jnp.float32)
            if first:
                accl[i] = kp
                accr[i] = pk
            else:
                accl[i] += kp
                accr[i] += pk

    add(c, True)

    def step(d, carry):
        if relay:
            src = lax.rem(c + mirror * d + ncol, ncol)
            @pl.when(jnp.logical_not(inner))
            def _():
                col_got(1, src)
                col_got(2, src)
        else:
            src = lax.rem(c + d, ncol)
            col_got(1, src)
            col_got(2, src)
        add(src, False)
        return carry

    lax.fori_loop(1, ncol, step, 0)

    for i in range(R):
        for h in range(H):
            re = accr[i, :B, h * 2 * B:(h + 1) * 2 * B]
            im = accr[i, B:, h * 2 * B:(h + 1) * 2 * B]
            first = jnp.where(low, re, pltpu.roll(im, B, 1))
            second = jnp.where(low, pltpu.roll(re, B, 1), im)
            for t, pk in ((2 * h, first), (2 * h + 1, second)):
                out_ref[i, t] = (accl[i, :, t * 2 * B:(t + 1) * 2 * B] - pk).astype(out_ref.dtype)

    for cp in sent:
        cp.wait_send()
    if relay:
        for n, (ok, peer) in enumerate(zip(has, step_to)):
            @pl.when(ok)
            def _(n=n, peer=peer):
                for kind in range(3):
                    pass_on(kind, c, n, peer).wait_send()

        @pl.when(inner)
        def _():
            for kind in range(3):
                for src, slot, peer in onward + last:
                    pass_on(kind, src, slot, peer).wait_send()


def per_device(nrow, ncol, k_blocks, p_blocks, k_columns, p_columns, molecule_order):
    R, S, B, W = p_blocks.shape
    G = molecule_order.shape[0] // ncol
    H = S // 2
    bf, i32 = jnp.bfloat16, jnp.int32
    vmem = pl.BlockSpec(memory_space=pltpu.VMEM)
    anywhere = pl.BlockSpec(memory_space=pltpu.HBM)
    dma = pltpu.SemaphoreType.DMA
    return pl.pallas_call(
        functools.partial(kernel, nrow, ncol, R, S, G),
        out_shape=jax.ShapeDtypeStruct(p_blocks.shape, bf),
        in_specs=[anywhere] * 5,
        out_specs=vmem,
        scratch_shapes=[
            pltpu.VMEM((nrow * R * S + 1, B, W), bf),
            pltpu.VMEM((2 * nrow * R * H + 1, B, W), bf),
            pltpu.VMEM((ncol, R * H, B, W), bf),
            pltpu.VMEM((ncol, R * H, 2 * B, W), bf),
            pltpu.VMEM((nrow + 1, 1, LANES), i32),
            pltpu.VMEM((ncol, 1, LANES), i32),
            pltpu.SMEM((nrow + 1, 1, LANES), i32),
            pltpu.SMEM((ncol, 1, LANES), i32),
            pltpu.SMEM((R * S,), i32),
            pltpu.VMEM((R, B, S * W), jnp.float32),
            pltpu.VMEM((R, 2 * B, S * B), jnp.float32),
            pltpu.SMEM((R, S), i32),
            pltpu.SMEM((R, S), i32),
            pltpu.SMEM(molecule_order.shape, i32),
            pltpu.VMEM((R, S, B, B), bf),
            *[dma((nrow,))] * 9,
            *[dma((ncol + 1,))] * 6,
            dma((5,)),
        ],
        compiler_params=pltpu.CompilerParams(
            collective_id=0, has_side_effects=True, vmem_limit_bytes=60 << 20),
    )(k_columns, p_columns, molecule_order, k_blocks,
      p_blocks.reshape(R * S, B, W))


def solution(mesh):
    in_specs = (
        P("row", "col", None, None),
        P("row", "col", None, None),
        P("row", "col"),
        P("row", "col"),
        P(),
    )
    out_specs = P("row", "col", None, None)
    body = functools.partial(per_device, mesh.shape["row"], mesh.shape["col"])
    return jax.shard_map(
        body, mesh=mesh, in_specs=in_specs, out_specs=out_specs, check_vma=False
    )
```

```python
import functools

import jax
import jax.numpy as jnp
from jax import lax
from jax.experimental import pallas as pl
from jax.experimental.pallas import tpu as pltpu
from jax.sharding import PartitionSpec as P

MESH = pl.DeviceIdType.MESH
LANES = 128
TAB = 8


def swap_halves(x):
    half = x.shape[-1] // 2
    return pltpu.roll(x.astype(jnp.float32), half, x.ndim - 1).astype(x.dtype)


def kernel(
    nrow, ncol, R, S, G,
    kc_ref, pc_ref, order_ref, k_ref, p_ref, out_ref,
    pbuf, kbuf, kcol, plcol, mrow, mcol, mrow_s, mcol_s, jout, accl, accr,
    kc, pc, order, kv,
    s_rp, r_rp, s_rk, r_rk, s_rm, r_rm, s_fm, s_fp, s_fk, s_ck, r_ck, s_cp, r_cp, s_cm, r_cm, lsem,
):
    r = lax.axis_index("row")
    c = lax.axis_index("col")
    H = S // 2
    PB = R * S
    KB = R * H
    SW = nrow * KB
    zero_p = nrow * PB
    zero_k = 2 * SW
    B = kv.shape[2]
    relay = ncol == 4

    rows = [lax.rem(r + d, nrow) for d in range(1, nrow)]
    cols = [lax.rem(c + d, ncol) for d in range(1, ncol)]
    core = lax.rem(r, 2)
    sibling = r + 1 - 2 * core
    same = [lax.rem(r + 2 * d, nrow) for d in range(1, nrow // 2)]
    other = [lax.rem(sibling + 2 * d, nrow) for d in range(1, nrow // 2)]

    barrier = pltpu.get_barrier_semaphore()
    near = same + [sibling] if relay else rows
    for peer in near:
        pl.semaphore_signal(barrier, inc=1, device_id={"row": peer}, device_id_type=MESH)
    if relay:
        inner = (c == 1) | (c == 2)
        mirror = jnp.where(c < 2, 1, -1)
        far = jnp.where(c == 1, 3, 0)
        has = (c < ncol - 1, c > 0)
        step_to = (c + 1, c - 1)
        arrivals = len(near) + jnp.where(inner, 2, 1)
        for ok, peer in zip(has, step_to):
            @pl.when(ok)
            def _(peer=peer):
                pl.semaphore_signal(barrier, inc=1, device_id={"col": peer}, device_id_type=MESH)
    else:
        arrivals = nrow + ncol - 2
        for peer in cols:
            pl.semaphore_signal(barrier, inc=1, device_id={"col": peer}, device_id_type=MESH)

    loads = [
        pltpu.make_async_copy(src, dst, lsem.at[n])
        for n, (src, dst) in enumerate((
            (kc_ref, kc), (pc_ref, pc), (order_ref, order), (k_ref, kv),
            (p_ref, pbuf.at[pl.ds(r * PB, PB)])))
    ]
    for cp in loads:
        cp.start()

    for cp in loads[:3]:
        cp.wait()

    lane = lax.broadcasted_iota(jnp.int32, (1, LANES), 1)
    meta = jnp.zeros((1, LANES), jnp.int32)
    orders = [order[c * G + j] for j in range(G)]
    krow, kcl, prow, pcl = [], [], [], []
    t_p, t_kl, t_kh = [], [], []
    for i in range(R):
        kcs = [kc[i, s] for s in range(S)]
        pcs = [pc[i, s] for s in range(S)]
        khit = [[kcs[s] == orders[j] for j in range(G)] for s in range(S)]
        phit = [[pcs[s] == orders[j] for j in range(G)] for s in range(S)]
        for s in range(S):
            for hit, a, b, out in ((khit, krow, kcl, False), (phit, prow, pcl, True)):
                pos_r = jnp.int32(nrow)
                pos_c = jnp.int32(0)
                col = jnp.int32(G)
                for j in range(G):
                    q = c * G + j
                    pos_r = jnp.where(hit[s][j], q // R, pos_r)
                    pos_c = jnp.where(hit[s][j], lax.rem(q, R) * TAB, pos_c)
                    col = jnp.where(hit[s][j], j, col)
                a.append(pos_r)
                b.append(pos_c)
                if out:
                    jout[i * S + s] = col
        for j in range(TAB):
            vp, vl, vh = jnp.int32(zero_p), jnp.int32(zero_k), jnp.int32(zero_k)
            if j < G:
                for s in range(S):
                    pair = (r * R + i) * H + s // 2
                    vp = jnp.where(phit[s][j], (r * R + i) * S + s, vp)
                    vl = jnp.where(khit[s][j], pair + (s % 2) * SW, vl)
                    vh = jnp.where(khit[s][j], pair + (1 - s % 2) * SW, vh)
            t_p.append(vp)
            t_kl.append(vl)
            t_kh.append(vh)
    entries = t_p + t_kl + t_kh + krow + kcl + prow + pcl
    for n, v in enumerate(entries):
        meta = jnp.where(lane == n, v, meta)
    O_KL, O_KH = R * TAB, 2 * R * TAB
    O_KR = 3 * R * TAB
    O_KC, O_PR, O_PC = O_KR + PB, O_KR + 2 * PB, O_KR + 3 * PB
    mrow[r] = meta
    mcol[c] = meta
    mrow[nrow] = jnp.where(lane < O_KL, zero_p, zero_k)

    for cp in loads[3:]:
        cp.wait()
    low = lax.broadcasted_iota(jnp.int32, (B, 2 * B), 1) < B
    for i in range(R):
        for h in range(H):
            pair = jnp.concatenate([kv[i, 2 * h], kv[i, 2 * h + 1]], axis=-1)
            kbuf[r * KB + i * H + h] = pair
            kcol[c, i * H + h] = pair
            a, b = pbuf[r * PB + i * S + 2 * h], pbuf[r * PB + i * S + 2 * h + 1]
            plcol[c, i * H + h, :B] = jnp.where(low, a, swap_halves(b))
            plcol[c, i * H + h, B:] = jnp.where(low, swap_halves(a), b)

    pl.semaphore_wait(barrier, arrivals)

    def row_copy(kind, src, send, peer):
        ref, recv = (
            (mrow.at[src], r_rm), (kbuf.at[pl.ds(src * KB, KB)], r_rk), (pbuf.at[pl.ds(src * PB, PB)], r_rp)
        )[kind]
        return pltpu.make_async_remote_copy(
            ref, ref, send, recv.at[src], device_id={"row": peer}, device_id_type=MESH)

    def col_copy(kind, src, send, peer):
        ref, recv = ((mcol, r_cm), (kcol, r_ck), (plcol, r_cp))[kind]
        return pltpu.make_async_remote_copy(
            ref.at[src], ref.at[src], send, recv.at[src], device_id={"col": peer}, device_id_type=MESH)

    def row_got(kind, src):
        row_copy(kind, src, s_rm.at[0], src).wait_recv()

    def col_got(kind, src):
        col_copy(kind, src, s_cm.at[0], src).wait_recv()

    sent = []

    def start(cp):
        cp.start()
        sent.append(cp)

    col_sems = (s_cm, s_ck, s_cp)

    def pass_on(kind, src, slot, peer):
        return col_copy(kind, src, col_sems[kind].at[slot], peer)

    if relay:
        for kind in range(3):
            for n, (ok, peer) in enumerate(zip(has, step_to)):
                @pl.when(ok)
                def _(kind=kind, n=n, peer=peer):
                    pass_on(kind, c, n, peer).start()
        for kind in range(3):
            for d, peer in enumerate(near):
                start(row_copy(kind, r, (s_rm, s_rk, s_rp)[kind].at[d], peer))
    else:
        for kind in range(3):
            for d, peer in enumerate(cols):
                start(pass_on(kind, c, d, peer))
            for d, peer in enumerate(same + [sibling] if kind else rows):
                start(row_copy(kind, r, (s_rm, s_rk, s_rp)[kind].at[d], peer))

    zero = jnp.zeros((B, 2 * B), jnp.bfloat16)
    pbuf[zero_p] = zero
    kbuf[zero_k] = zero

    def swapped(src):
        for n in range(KB):
            kbuf[SW + src * KB + n] = swap_halves(kbuf[src * KB + n])

    swapped(r)

    def inside(kinds, hops):
        if relay:
            @pl.when(inner)
            def _():
                for kind in kinds:
                    for src, slot, peer in hops:
                        col_got(kind, src)
                        pass_on(kind, src, slot, peer).start()

    if relay:
        onward = [(c - 1, 2, c + 1), (c + 1, 3, c - 1)]
        last = [(far, 4, c - mirror)]
    else:
        onward = last = []
    inside((0, 1), onward)
    for d, src in enumerate(same):
        if relay:
            row_got(0, src)
            start(row_copy(0, src, s_fm.at[d], sibling))
        row_got(1, src)
        start(row_copy(1, src, s_fk.at[d], sibling))
    inside((2,), onward)
    for src in same:
        swapped(src)
    inside((0, 1), last)
    for d, src in enumerate(same):
        row_got(2, src)
        start(row_copy(2, src, s_fp.at[d], sibling))
    inside((2,), last)
    for src in [sibling] + other:
        row_got(1, src)
        swapped(src)
    for src in [sibling] + other:
        row_got(2, src)

    for src in [sibling] + other if relay else rows:
        row_got(0, src)
    if relay:
        @pl.when(jnp.logical_not(inner))
        def _():
            for d in range(1, ncol):
                col_got(0, c + mirror * d)
    else:
        for src in cols:
            col_got(0, src)
    tables = [pltpu.make_async_copy(mrow, mrow_s, lsem.at[0]), pltpu.make_async_copy(mcol, mcol_s, lsem.at[1])]
    for cp in tables:
        cp.start()
    for cp in tables:
        cp.wait()

    def add(g, first):
        for i in range(R):
            outs = [jout[i * S + t] for t in range(S)]
            right, right_k = [], []
            for s in range(S):
                qr, qc = mcol_s[g, 0, O_KR + i * S + s], mcol_s[g, 0, O_KC + i * S + s]
                right.append(jnp.concatenate(
                    [pbuf[mrow_s[qr, 0, qc + outs[t]]] for t in range(S)], axis=1))
                qr, qc = mcol_s[g, 0, O_PR + i * S + s], mcol_s[g, 0, O_PC + i * S + s]
                right_k.append(jnp.concatenate([
                    jnp.where(low,
                              kbuf[mrow_s[qr, 0, qc + outs[2 * h] + O_KL]],
                              kbuf[mrow_s[qr, 0, qc + outs[2 * h + 1] + O_KH]])
                    for h in range(H)], axis=1))
            left = jnp.concatenate([kcol[g, i * H + h] for h in range(H)], axis=1)
            kp = jnp.dot(left, jnp.concatenate(right, axis=0), preferred_element_type=jnp.float32)
            left = jnp.concatenate([plcol[g, i * H + h] for h in range(H)], axis=1)
            pk = jnp.dot(left, jnp.concatenate(right_k, axis=0), preferred_element_type=jnp.float32)
            if first:
                accl[i] = kp
                accr[i] = pk
            else:
                accl[i] += kp
                accr[i] += pk

    add(c, True)

    def step(d, carry):
        if relay:
            src = lax.rem(c + mirror * d + ncol, ncol)
            @pl.when(jnp.logical_not(inner))
            def _():
                col_got(1, src)
                col_got(2, src)
        else:
            src = lax.rem(c + d, ncol)
            col_got(1, src)
            col_got(2, src)
        add(src, False)
        return carry

    lax.fori_loop(1, ncol, step, 0)

    for i in range(R):
        for h in range(H):
            re = accr[i, :B, h * 2 * B:(h + 1) * 2 * B]
            im = accr[i, B:, h * 2 * B:(h + 1) * 2 * B]
            first = jnp.where(low, re, pltpu.roll(im, B, 1))
            second = jnp.where(low, pltpu.roll(re, B, 1), im)
            for t, pk in ((2 * h, first), (2 * h + 1, second)):
                out_ref[i, t] = (accl[i, :, t * 2 * B:(t + 1) * 2 * B] - pk).astype(out_ref.dtype)

    for cp in sent:
        cp.wait_send()
    if relay:
        for n, (ok, peer) in enumerate(zip(has, step_to)):
            @pl.when(ok)
            def _(n=n, peer=peer):
                for kind in range(3):
                    pass_on(kind, c, n, peer).wait_send()

        @pl.when(inner)
        def _():
            for kind in range(3):
                for src, slot, peer in onward + last:
                    pass_on(kind, src, slot, peer).wait_send()


def per_device(nrow, ncol, k_blocks, p_blocks, k_columns, p_columns, molecule_order):
    R, S, B, W = p_blocks.shape
    G = molecule_order.shape[0] // ncol
    H = S // 2
    bf, i32 = jnp.bfloat16, jnp.int32
    vmem = pl.BlockSpec(memory_space=pltpu.VMEM)
    anywhere = pl.BlockSpec(memory_space=pltpu.HBM)
    dma = pltpu.SemaphoreType.DMA
    return pl.pallas_call(
        functools.partial(kernel, nrow, ncol, R, S, G),
        out_shape=jax.ShapeDtypeStruct(p_blocks.shape, bf),
        in_specs=[anywhere] * 5,
        out_specs=vmem,
        scratch_shapes=[
            pltpu.VMEM((nrow * R * S + 1, B, W), bf),
            pltpu.VMEM((2 * nrow * R * H + 1, B, W), bf),
            pltpu.VMEM((ncol, R * H, B, W), bf),
            pltpu.VMEM((ncol, R * H, 2 * B, W), bf),
            pltpu.VMEM((nrow + 1, 1, LANES), i32),
            pltpu.VMEM((ncol, 1, LANES), i32),
            pltpu.SMEM((nrow + 1, 1, LANES), i32),
            pltpu.SMEM((ncol, 1, LANES), i32),
            pltpu.SMEM((R * S,), i32),
            pltpu.VMEM((R, B, S * W), jnp.float32),
            pltpu.VMEM((R, 2 * B, S * B), jnp.float32),
            pltpu.SMEM((R, S), i32),
            pltpu.SMEM((R, S), i32),
            pltpu.SMEM(molecule_order.shape, i32),
            pltpu.VMEM((R, S, B, B), bf),
            *[dma((nrow,))] * 9,
            *[dma((ncol + 1,))] * 6,
            dma((5,)),
        ],
        compiler_params=pltpu.CompilerParams(
            collective_id=0, has_side_effects=True, vmem_limit_bytes=60 << 20),
    )(k_columns, p_columns, molecule_order, k_blocks,
      p_blocks.reshape(R * S, B, W))


def solution(mesh):
    in_specs = (
        P("row", "col", None, None),
        P("row", "col", None, None),
        P("row", "col"),
        P("row", "col"),
        P(),
    )
    out_specs = P("row", "col", None, None)
    body = functools.partial(per_device, mesh.shape["row"], mesh.shape["col"])
    return jax.shard_map(
        body, mesh=mesh, in_specs=in_specs, out_specs=out_specs, check_vma=False
    )
```
